32 devices in a mesh: groups: 2 (over y), pfx: 4 (over z), smp: 2 (over x), kv: 2 (over core).
Axes of the slice: x: 2, y: 2, z: 4, core: 2. Of those that a mesh axis runs over, the one named last changes fastest.
Arguments:
- hidden: bfloat16 [64, 8192], P(('groups', 'smp'), 'pfx'), parts along dimension 0, may hold values from -6 to 6
- norm_gain: bfloat16 [8192], P('pfx'), may hold values from 0.5 to 1.5
- query_weight: bfloat16 [8192, 4096], P('pfx', 'kv'), may hold values from -0.0625 to 0.0625
- key_matrix: bfloat16 [8192, 512], P('pfx', 'kv'), may hold values from -0.52734375 to 0.52734375
- value_matrix: bfloat16 [8192, 512], P('pfx', 'kv'), may hold values from -0.0625 to 0.0625
- prefix_key: bfloat16 [16384, 512], P(('groups', 'pfx', 'smp'), 'kv'), parts along dimension 0, may hold values from -160 to 160
- shared_prefix_value: bfloat16 [16384, 512], P(('groups', 'pfx', 'smp'), 'kv'), parts along dimension 0, may hold values from -6 to 6
- sample_suffix_key: bfloat16 [64, 128, 512], P(('groups', 'smp'), 'pfx', 'kv'), parts along dimension 0, may hold values from -24 to 24
- sample_suffix_value: bfloat16 [64, 128, 512], P(('groups', 'smp'), 'pfx', 'kv'), parts along dimension 0, may hold values from -6 to 6
- lengths: int32 [64], P(('groups', 'smp')), parts along dimension 0, may hold values from 1 to 128, as said below
- assign: int32 [64], P(('groups', 'smp')), parts along dimension 0, may hold values from 0 to 31, as said below
Outputs:
- attended: bfloat16 [64, 4096], P(('groups', 'smp'), 'kv'), parts along dimension 0
The draws below stay inside these ranges and needn't reach their ends.
There are 2 independent parts, one for each index of `groups`. The reference program is written for one: setup_inputs(seed, part) draws one part's arguments, and reference() takes and returns one part's arrays. A program takes and returns all parts, laid end to end along the dimension named above; an argument that names none is the same for every part. Nothing has to cross between parts.
Inputs may be any that keep to these rules, and one draw needn't show every extreme that they name: `lengths`: some sample has exactly 128 live positions. `assign`: each aligned block of 16 rows holds each sample number of that block once.
All inputs are finite; a program needn't handle non-finite values.
Results may differ from the reference program's by a relative error of at most 0.017.
Values may be sent and summed in bfloat16 or wider, within the bound.
No kernel may reach another device: no remote copies, remote signals or barrier semaphores. Data moves between devices by JAX's collectives and lax.ppermute only.
A program may use at most 64 MiB of HBM per device.

```python
import jax
import jax.numpy as jnp
from jax import lax

MODEL_WIDTH = 8192
HEAD_WIDTH = 128
QUERY_HEADS = 32
KEY_VALUE_HEADS = 4
B_DEV = 16
SAMPLE_TOTAL = 32
PREFIX_LENGTH = 8192
SUFFIX_LENGTH = 128


def draw_prefix_key(key, part):
    starting_keys = jnp.clip(3.0 * jax.random.normal(key, (PREFIX_LENGTH, KEY_VALUE_HEADS * HEAD_WIDTH), jnp.float32), -48.0, 48.0)
    return starting_keys.astype(jnp.bfloat16)


def draw_lengths(key, part):
    length_draw = jax.random.randint(key, (SAMPLE_TOTAL,), 1, SUFFIX_LENGTH + 1)
    spot_index = jax.random.randint(jax.random.fold_in(key, 21), (), 0, SAMPLE_TOTAL)
    return length_draw.at[spot_index].set(SUFFIX_LENGTH).astype(jnp.int32)


def draw_assign(key, part):
    block_count = SAMPLE_TOTAL // B_DEV
    block_keys = jax.random.split(key, block_count)
    block_orders = jax.vmap(lambda block_key: jax.random.permutation(block_key, B_DEV))(block_keys)
    offsets = jnp.arange(block_count, dtype=jnp.int32)[:, None] * B_DEV
    return (block_orders.astype(jnp.int32) + offsets).reshape(SAMPLE_TOTAL)


def block_scale(key, shape, cuts, smallest, largest):
    gain = 1.0
    for dim, blocks in cuts:
        steps = jax.random.uniform(jax.random.fold_in(jax.random.fold_in(key, 6), dim), (blocks,), jnp.float32, smallest / len(cuts), largest / len(cuts))
        gain = gain * jnp.repeat(jnp.exp(steps), shape[dim] // blocks).reshape((-1,) + (1,) * (len(shape) - 1 - dim))
    return gain


def normal_values(key, shape, scale, reach, shards=(), kind=jnp.bfloat16):
    drawn = jax.random.normal(key, shape, jnp.float32) * scale
    if len(shards) > 0:
        drawn = block_scale(key, shape, shards, -0.22, 0.18) * drawn
    return jnp.clip(drawn, min=-reach, max=reach).astype(kind)


def setup_inputs(seed: int = 0, part: int = 0) -> dict:
    key_of = jax.random.split(jax.random.key(seed), 12)
    part_keys = jax.random.split(jax.random.fold_in(key_of[11], part), 12)
    hidden = normal_values(part_keys[0], (SAMPLE_TOTAL, MODEL_WIDTH), 1.0, 6.0, ((0, 2), (1, 4)))
    norm_gain = jnp.clip(1.0 + 0.1 * jax.random.normal(key_of[1], (MODEL_WIDTH,), jnp.float32), 0.5, 1.5).astype(jnp.bfloat16)
    query_weight = normal_values(key_of[2], (MODEL_WIDTH, QUERY_HEADS * HEAD_WIDTH), MODEL_WIDTH ** -0.5, 0.0625, ((0, 4), (1, 2)))
    key_matrix = normal_values(key_of[3], (MODEL_WIDTH, KEY_VALUE_HEADS * HEAD_WIDTH), (8.0 / MODEL_WIDTH ** 0.5), 0.52734375, ((0, 4), (1, 2)))
    value_matrix = normal_values(key_of[4], (MODEL_WIDTH, KEY_VALUE_HEADS * HEAD_WIDTH), MODEL_WIDTH ** -0.5, 0.0625, ((0, 4), (1, 2)))
    prefix_key = draw_prefix_key(jax.random.fold_in(jax.random.fold_in(key_of[11], part), 71), part)
    shared_prefix_value = normal_values(part_keys[6], (PREFIX_LENGTH, KEY_VALUE_HEADS * HEAD_WIDTH), 1.0, 6.0, ((0, 8), (1, 2)))
    sample_suffix_key = normal_values(part_keys[7], (SAMPLE_TOTAL, SUFFIX_LENGTH, KEY_VALUE_HEADS * HEAD_WIDTH), 4.0, 24.0, ((0, 2), (1, 4), (2, 2)))
    sample_suffix_value = normal_values(part_keys[8], (SAMPLE_TOTAL, SUFFIX_LENGTH, KEY_VALUE_HEADS * HEAD_WIDTH), 1.0, 6.0, ((0, 2), (1, 4), (2, 2)))
    lengths = draw_lengths(jax.random.fold_in(jax.random.fold_in(key_of[11], part), 71), part)
    assign = draw_assign(jax.random.fold_in(jax.random.fold_in(key_of[11], part), 71), part)
    return dict(hidden=hidden, norm_gain=norm_gain, query_weight=query_weight, key_matrix=key_matrix, value_matrix=value_matrix, prefix_key=prefix_key, shared_prefix_value=shared_prefix_value, sample_suffix_key=sample_suffix_key, sample_suffix_value=sample_suffix_value, lengths=lengths, assign=assign)


norm_eps = 1e-05
very_negative = -1e+30

def project(normed, weight, rms_value):
    product = jnp.dot(normed, weight, preferred_element_type=jnp.float32)
    return (product / rms_value[:, None]).astype(jnp.bfloat16)

def reference(hidden, norm_gain, query_weight, key_matrix, value_matrix, prefix_key, shared_prefix_value, sample_suffix_key, sample_suffix_value, lengths, assign):
    hidden_wide = hidden.astype(jnp.float32)
    rms_value = jnp.sqrt(lax.optimization_barrier(jnp.sum(hidden_wide * hidden_wide, axis=1)) / MODEL_WIDTH + norm_eps)
    normed = (hidden_wide * norm_gain.astype(jnp.float32)).astype(jnp.bfloat16)
    query_rows = project(normed, query_weight, rms_value)
    new_key = project(normed, key_matrix, rms_value)
    new_value = project(normed, value_matrix, rms_value)
    slot_length = jnp.take(lengths, assign, axis=0)
    slot_keys = jnp.take(sample_suffix_key, assign, axis=0)
    slot_values = jnp.take(sample_suffix_value, assign, axis=0)
    live_mask = jnp.arange(SUFFIX_LENGTH, dtype=jnp.int32)[None, :] < slot_length[:, None]
    group_width = QUERY_HEADS // KEY_VALUE_HEADS
    score_scale = HEAD_WIDTH ** (-0.5)

    def one_head(head_index):
        group_index = head_index // group_width
        head_query = lax.dynamic_slice_in_dim(query_rows, head_index * HEAD_WIDTH, HEAD_WIDTH, 1)
        prefix_keys = lax.dynamic_slice_in_dim(prefix_key, group_index * HEAD_WIDTH, HEAD_WIDTH, 1)
        prefix_values = lax.dynamic_slice_in_dim(shared_prefix_value, group_index * HEAD_WIDTH, HEAD_WIDTH, 1)
        suffix_keys = lax.dynamic_slice_in_dim(slot_keys, group_index * HEAD_WIDTH, HEAD_WIDTH, 2).astype(jnp.float32)
        suffix_values = lax.dynamic_slice_in_dim(slot_values, group_index * HEAD_WIDTH, HEAD_WIDTH, 2).astype(jnp.float32)
        own_key = lax.dynamic_slice_in_dim(new_key, group_index * HEAD_WIDTH, HEAD_WIDTH, 1).astype(jnp.float32)
        own_value = lax.dynamic_slice_in_dim(new_value, group_index * HEAD_WIDTH, HEAD_WIDTH, 1).astype(jnp.float32)
        query_wide = head_query.astype(jnp.float32)
        prefix_scores = jnp.dot(head_query, prefix_keys.T, preferred_element_type=jnp.float32) * score_scale
        suffix_scores = jnp.einsum('bd,bsd->bs', query_wide, suffix_keys, precision=lax.Precision.HIGHEST) * score_scale
        suffix_scores = jnp.where(live_mask, suffix_scores, very_negative)
        own_score = lax.optimization_barrier(jnp.sum(query_wide * own_key, axis=1)) * score_scale
        top_score = jnp.maximum(jnp.maximum(lax.optimization_barrier(jnp.max(prefix_scores, axis=1)), lax.optimization_barrier(jnp.max(suffix_scores, axis=1))), own_score)
        prefix_weights = jnp.exp(prefix_scores - top_score[:, None]).astype(jnp.bfloat16)
        suffix_weights = jnp.where(live_mask, jnp.exp(suffix_scores - top_score[:, None]), 0.0).astype(jnp.bfloat16)
        own_weight = lax.optimization_barrier(jnp.exp(own_score - top_score).astype(jnp.bfloat16)).astype(jnp.float32)
        denominator = lax.optimization_barrier(jnp.sum(prefix_weights.astype(jnp.float32), axis=1)) + lax.optimization_barrier(jnp.sum(suffix_weights.astype(jnp.float32), axis=1)) + own_weight
        numerator = jnp.dot(prefix_weights, prefix_values, preferred_element_type=jnp.float32)
        numerator = numerator + jnp.einsum('bs,bsd->bd', suffix_weights.astype(jnp.float32), suffix_values, precision=lax.Precision.HIGHEST)
        numerator = numerator + own_weight[:, None] * own_value
        return (numerator / denominator[:, None]).astype(jnp.bfloat16)
    heads = lax.map(one_head, jnp.arange(QUERY_HEADS, dtype=jnp.int32))
    return jnp.transpose(heads, (1, 0, 2)).reshape(SAMPLE_TOTAL, QUERY_HEADS * HEAD_WIDTH)
```

```python
import jax
import jax.numpy as jnp
from jax import lax
from jax.experimental import pallas as pl
from jax.experimental.pallas import tpu as pltpu
from jax.sharding import PartitionSpec as P

HEAD_WIDTH = 128
LANES = 128
norm_eps = 1e-05
very_negative = -1e30
score_scale = HEAD_WIDTH ** (-0.5)
bf16 = jnp.bfloat16
f32 = jnp.float32

ANY = pl.BlockSpec(memory_space=pl.ANY)
VMEM = pl.BlockSpec(memory_space=pltpu.VMEM)
SMEM = pl.BlockSpec(memory_space=pltpu.SMEM)


def start_copies(sources, targets, sems):
    copies = [
        pltpu.make_async_copy(source, target, sems.at[place])
        for place, (source, target) in enumerate(zip(sources, targets))
    ]
    for copy in copies:
        copy.start()
    return copies


def project(hidden, norm_gain, query_weight, key_matrix, value_matrix, chunks):
    rows, width = hidden.shape
    query_width = query_weight.shape[1]
    kv_width = key_matrix.shape[1]
    total = query_width + 2 * kv_width + LANES
    depth = width // chunks

    def kernel(hidden_in, gain_in, wq_in, wk_in, wv_in, out, hidden_v, gain_v, wq, wk, wv, sems):
        small = start_copies((hidden_in, gain_in), (hidden_v, gain_v), sems)
        large = []
        for chunk in range(chunks):
            part = pl.ds(chunk * depth, depth)
            large.append(
                start_copies(
                    (wq_in.at[part], wk_in.at[part], wv_in.at[part]),
                    (wq.at[part], wk.at[part], wv.at[part]),
                    sems.at[pl.ds(2 + 3 * chunk, 3)],
                )
            )
        for copy in small:
            copy.wait()
        wide = hidden_v[...].astype(f32)
        squares = jnp.sum(wide * wide, axis=1, keepdims=True)
        out[:, query_width + 2 * kv_width :] = jnp.broadcast_to(squares, (rows, LANES))
        normed = (wide * gain_v[...].astype(f32)).astype(bf16)
        for chunk in range(chunks):
            for copy in large[chunk]:
                copy.wait()
            part = pl.ds(chunk * depth, depth)
            left = normed[:, chunk * depth : (chunk + 1) * depth]
            place = 0
            for weight in (wq, wk, wv):
                columns = weight.shape[1]
                value = jnp.dot(left, weight[part], preferred_element_type=f32)
                if chunk == 0:
                    out[:, place : place + columns] = value
                else:
                    out[:, place : place + columns] += value
                place += columns

    return pl.pallas_call(
        kernel,
        in_specs=[ANY] * 5,
        out_specs=VMEM,
        out_shape=jax.ShapeDtypeStruct((rows, total), f32),
        scratch_shapes=[
            pltpu.VMEM(hidden.shape, bf16),
            pltpu.VMEM((1, width), bf16),
            pltpu.VMEM(query_weight.shape, bf16),
            pltpu.VMEM(key_matrix.shape, bf16),
            pltpu.VMEM(value_matrix.shape, bf16),
            pltpu.SemaphoreType.DMA((2 + 3 * chunks,)),
        ],
        compiler_params=pltpu.CompilerParams(vmem_limit_bytes=60 << 20),
        cost_estimate=pl.CostEstimate(
            flops=2 * rows * width * total, bytes_accessed=2 * width * total, transcendentals=0
        ),
        name="project",
    )(hidden, norm_gain.reshape(1, width), query_weight, key_matrix, value_matrix)


def scores_of(queries, keys):
    return (
        lax.dot_general(queries, keys, (((1,), (1,)), ((), ())), preferred_element_type=f32)
        * score_scale
    )


def own_attention(parts, keys, values, suffix_keys, suffix_values, lengths, assign, sizes):
    rows, query_width, kv_width, model_width, suffix_len = sizes
    kv_heads = kv_width // HEAD_WIDTH
    group = query_width // kv_width
    tall = group * rows
    count = len(parts)
    prefix = keys.shape[0]
    suffix = suffix_keys.shape[0]

    def kernel(*refs):
        part_in = refs[:count]
        k_in, v_in, ks_in, vs_in, len_s, assign_s = refs[count : count + 6]
        q_out, acc_out, top_out, sum_out = refs[count + 6 : count + 10]
        part_v, k_v, v_v, ks_v, vs_v, sems = refs[count + 10 :]
        copies = start_copies(
            (*part_in, k_in, ks_in, v_in, vs_in),
            (*(part_v.at[i] for i in range(count)), k_v, ks_v, v_v, vs_v),
            sems,
        )
        first = lax.axis_index("pfx") == 0
        row_base = lax.axis_index("smp") * rows
        position_base = lax.axis_index("pfx") * suffix_len
        slot_of = lax.broadcasted_iota(jnp.int32, (rows, suffix), 1) // suffix_len
        place_of = lax.broadcasted_iota(jnp.int32, (rows, suffix), 1) % suffix_len + position_base
        row_of = lax.broadcasted_iota(jnp.int32, (rows, suffix), 0)
        live_len = jnp.zeros((rows, suffix), jnp.int32)
        row_slot = jnp.zeros((rows, suffix), jnp.int32)
        for i in range(rows):
            live_len = jnp.where(slot_of == i, len_s[i], live_len)
            row_slot = jnp.where(row_of == i, assign_s[i] - row_base, row_slot)
        live = (slot_of == row_slot) & (place_of < live_len)
        bias = jnp.where(live, 0.0, very_negative)
        bias = jnp.concatenate([bias] * group, axis=0)
        for copy in copies[:count]:
            copy.wait()
        total = part_v[0]
        for i in range(1, count):
            total = total + part_v[i]
        squares = total[:, query_width + 2 * kv_width :][:, :1]
        rms = jnp.sqrt(squares / model_width + norm_eps)
        projected = (total[:, : query_width + 2 * kv_width] / rms).astype(bf16)
        for copy in copies[count : count + 2]:
            copy.wait()
        for g in range(kv_heads):
            lanes = slice(g * HEAD_WIDTH, (g + 1) * HEAD_WIDTH)
            base = g * group * HEAD_WIDTH
            queries = jnp.concatenate(
                [
                    projected[:, base + h * HEAD_WIDTH : base + (h + 1) * HEAD_WIDTH]
                    for h in range(group)
                ],
                axis=0,
            )
            q_out[g] = queries
            key_at = query_width + g * HEAD_WIDTH
            value_at = key_at + kv_width
            new_key = projected[:, key_at : key_at + HEAD_WIDTH].astype(f32)
            new_value = projected[:, value_at : value_at + HEAD_WIDTH].astype(f32)
            new_key = jnp.concatenate([new_key] * group, axis=0)
            new_value = jnp.concatenate([new_value] * group, axis=0)
            own = jnp.sum(queries.astype(f32) * new_key, axis=1, keepdims=True) * score_scale
            own = jnp.where(first, own, very_negative)
            near = scores_of(queries, k_v[:, lanes])
            far = scores_of(queries, ks_v[:, lanes])
            far = jnp.where(bias < 0.0, very_negative, far)
            top = jnp.maximum(
                jnp.max(near, axis=1, keepdims=True), jnp.max(far, axis=1, keepdims=True)
            )
            top = jnp.maximum(top, own)
            near_weight = jnp.exp(near - top).astype(bf16)
            far_weight = jnp.where(bias < 0.0, 0.0, jnp.exp(far - top)).astype(bf16)
            own_weight = jnp.where(first, jnp.exp(own - top), 0.0).astype(bf16).astype(f32)
            if g == 0:
                for copy in copies[count + 2 :]:
                    copy.wait()
            acc = jnp.dot(near_weight, v_v[:, lanes], preferred_element_type=f32)
            acc += jnp.dot(far_weight, vs_v[:, lanes], preferred_element_type=f32)
            acc_out[g] = acc + own_weight * new_value
            denominator = (
                jnp.sum(near_weight.astype(f32), axis=1, keepdims=True)
                + jnp.sum(far_weight.astype(f32), axis=1, keepdims=True)
                + own_weight
            )
            top_out[g] = jnp.broadcast_to(top, (tall, LANES))
            sum_out[g] = jnp.broadcast_to(denominator, (tall, LANES))

    state = jax.ShapeDtypeStruct((kv_heads, tall, LANES), f32)
    return pl.pallas_call(
        kernel,
        in_specs=[ANY] * (count + 4) + [SMEM] * 2,
        out_specs=[VMEM] * 4,
        out_shape=[
            jax.ShapeDtypeStruct((kv_heads, tall, HEAD_WIDTH), bf16),
            state,
            state,
            state,
        ],
        scratch_shapes=[
            pltpu.VMEM((count, *parts[0].shape), f32),
            pltpu.VMEM(keys.shape, bf16),
            pltpu.VMEM(values.shape, bf16),
            pltpu.VMEM(suffix_keys.shape, bf16),
            pltpu.VMEM(suffix_values.shape, bf16),
            pltpu.SemaphoreType.DMA((count + 4,)),
        ],
        compiler_params=pltpu.CompilerParams(vmem_limit_bytes=32 << 20),
        cost_estimate=pl.CostEstimate(
            flops=4 * kv_heads * tall * (prefix + suffix) * HEAD_WIDTH,
            bytes_accessed=4 * (prefix + suffix) * kv_width,
            transcendentals=kv_heads * tall * (prefix + suffix),
        ),
        name="own_attention",
    )(*parts, keys, values, suffix_keys, suffix_values, lengths, assign)


def far_attention(queries, acc, top, denominator, keys, values, rows):
    kv_heads, tall, _ = queries.shape
    group = tall // rows
    heads = kv_heads * group
    count = len(keys)
    width = heads * HEAD_WIDTH

    def kernel(*refs):
        q_in, acc_in, top_in, sum_in = refs[:4]
        k_in = refs[4 : 4 + count]
        v_in = refs[4 + count : 4 + 2 * count]
        out = refs[4 + 2 * count]
        k_v, v_v, sems = refs[5 + 2 * count :]
        copies = start_copies(
            (*k_in, *v_in),
            (*(k_v.at[i] for i in range(count)), *(v_v.at[i] for i in range(count))),
            sems,
        )
        lane = lax.broadcasted_iota(jnp.int32, (rows, LANES), 1)
        stats = jnp.zeros((rows, LANES), f32)
        for copy in copies[:count]:
            copy.wait()
        for g in range(kv_heads):
            lanes = slice(g * HEAD_WIDTH, (g + 1) * HEAD_WIDTH)
            scores = [scores_of(q_in[g], k_v[i, :, lanes]) for i in range(count)]
            old_top = top_in[g]
            new_top = old_top
            for score in scores:
                new_top = jnp.maximum(new_top, jnp.max(score, axis=1, keepdims=True))
            top_high = new_top.astype(bf16).astype(f32)
            top_low = (new_top - top_high).astype(bf16).astype(f32)
            new_top = top_high + top_low
            factor = jnp.exp(old_top - new_top)
            total = acc_in[g] * factor
            weight_sum = sum_in[g] * factor
            if g == 0:
                for copy in copies[count:]:
                    copy.wait()
            for i, score in enumerate(scores):
                weight = jnp.exp(score - new_top[:, :1]).astype(bf16)
                total += jnp.dot(weight, v_v[i, :, lanes], preferred_element_type=f32)
                weight_sum += jnp.sum(weight.astype(f32), axis=1, keepdims=True)
            sum_high = weight_sum.astype(bf16).astype(f32)
            sum_low = weight_sum - sum_high
            for h in range(group):
                head = g * group + h
                part = slice(h * rows, (h + 1) * rows)
                out[:, head * HEAD_WIDTH : (head + 1) * HEAD_WIDTH] = total[part].astype(bf16)
                for k, value in enumerate((top_high, top_low, sum_high, sum_low)):
                    stats = jnp.where(lane == k * heads + head, value[part], stats)
        out[:, width:] = stats.astype(bf16)

    return pl.pallas_call(
        kernel,
        in_specs=[VMEM] * 4 + [ANY] * (2 * count),
        out_specs=VMEM,
        out_shape=jax.ShapeDtypeStruct((rows, width + LANES), bf16),
        scratch_shapes=[
            pltpu.VMEM((count, *keys[0].shape), bf16),
            pltpu.VMEM((count, *values[0].shape), bf16),
            pltpu.SemaphoreType.DMA((2 * count,)),
        ],
        compiler_params=pltpu.CompilerParams(vmem_limit_bytes=32 << 20),
        cost_estimate=pl.CostEstimate(
            flops=4 * kv_heads * tall * count * keys[0].shape[0] * HEAD_WIDTH,
            bytes_accessed=4 * count * keys[0].size,
            transcendentals=kv_heads * tall * count * keys[0].shape[0],
        ),
        name="far_attention",
    )(queries, acc, top, denominator, *keys, *values)


def combine(messages, heads):
    rows, wide = messages[0].shape
    width = wide - LANES
    count = len(messages)

    def kernel(*refs):
        message_in = refs[:count]
        out = refs[count]
        message_v, sems = refs[count + 1 :]
        copies = start_copies(message_in, [message_v.at[i] for i in range(count)], sems)
        for copy in copies:
            copy.wait()
        tops, sums = [], []
        for i in range(count):
            stats = message_v[i, :, width:].astype(f32)
            pair = stats + pltpu.roll(stats, LANES - heads, 1)
            tops.append(pair)
            sums.append(pltpu.roll(pair, LANES - 2 * heads, 1))
        top = tops[0]
        for i in range(1, count):
            top = jnp.maximum(top, tops[i])
        live = lax.broadcasted_iota(jnp.int32, (rows, LANES), 1) < heads
        factors = [jnp.where(live, jnp.exp(tops[i] - top), 0.0) for i in range(count)]
        denominator = factors[0] * sums[0]
        for i in range(1, count):
            denominator += factors[i] * sums[i]
        denominator = jnp.where(live, denominator, 1.0)
        scales = [factor / denominator for factor in factors]
        for h in range(heads):
            part = slice(h * HEAD_WIDTH, (h + 1) * HEAD_WIDTH)
            total = scales[0][:, h : h + 1] * message_v[0, :, part].astype(f32)
            for i in range(1, count):
                total += scales[i][:, h : h + 1] * message_v[i, :, part].astype(f32)
            out[:, part] = total.astype(bf16)

    return pl.pallas_call(
        kernel,
        in_specs=[ANY] * count,
        out_specs=VMEM,
        out_shape=jax.ShapeDtypeStruct((rows, width), bf16),
        scratch_shapes=[
            pltpu.VMEM((count, rows, wide), bf16),
            pltpu.SemaphoreType.DMA((count,)),
        ],
        compiler_params=pltpu.CompilerParams(vmem_limit_bytes=32 << 20),
        name="combine",
    )(*messages)


def shifted(value, axis, step):
    size = lax.axis_size(axis)
    if size & (size - 1):
        pairs = [(i, (i + step) % size) for i in range(size)]
    else:
        pairs = [(i, i ^ step) for i in range(size)]
    return lax.ppermute(value, axis, pairs)


def exchanged(value, axis):
    return [shifted(value, axis, step) for step in range(1, lax.axis_size(axis))]


def body(
    hidden,
    norm_gain,
    query_weight,
    key_matrix,
    value_matrix,
    prefix_key,
    shared_prefix_value,
    sample_suffix_key,
    sample_suffix_value,
    lengths,
    assign,
):
    rows, width = hidden.shape
    query_width = query_weight.shape[1]
    kv_width = key_matrix.shape[1]
    heads = query_width // HEAD_WIDTH
    suffix_len = sample_suffix_key.shape[1]
    direct = lax.axis_size("pfx") <= 4
    far_keys = exchanged(prefix_key, "smp")
    far_values = exchanged(shared_prefix_value, "smp")
    partial = project(hidden, norm_gain, query_weight, key_matrix, value_matrix, 4)
    if direct:
        parts = [partial] + exchanged(partial, "pfx")
    else:
        parts = [lax.psum(partial, "pfx")]
    sizes = (rows, query_width, kv_width, width * lax.axis_size("pfx"), suffix_len)
    queries, acc, top, denominator = own_attention(
        parts,
        prefix_key,
        shared_prefix_value,
        sample_suffix_key.reshape(-1, kv_width),
        sample_suffix_value.reshape(-1, kv_width),
        lengths,
        assign,
        sizes,
    )
    message = far_attention(queries, acc, top, denominator, far_keys, far_values, rows)
    if direct:
        messages = [message] + exchanged(message, "pfx")
    else:
        gathered = lax.all_gather(message, "pfx", axis=0)
        messages = [gathered[i] for i in range(lax.axis_size("pfx"))]
    return combine(messages, heads)


def solution(mesh):
    return jax.shard_map(
        body,
        mesh=mesh,
        in_specs=(
            P(("groups", "smp"), "pfx"),
            P("pfx"),
            P("pfx", "kv"),
            P("pfx", "kv"),
            P("pfx", "kv"),
            P(("groups", "pfx", "smp"), "kv"),
            P(("groups", "pfx", "smp"), "kv"),
            P(("groups", "smp"), "pfx", "kv"),
            P(("groups", "smp"), "pfx", "kv"),
            P(("groups", "smp")),
            P(("groups", "smp")),
        ),
        out_specs=P(("groups", "smp"), "kv"),
        check_vma=False,
    )
```
